256 devices in a mesh: group: 8 (over y, x_lo), dom: 32 (over z, x_hi, core).
Axes of the slice: x: 4 (x_hi: 2, x_lo: 2; x = x_hi * 2 + x_lo), y: 4, z: 8, core: 2. Of those that a mesh axis runs over, the one named last changes fastest.
Arguments:
- feats: bfloat16 [524288, 128], P(('group', 'dom')), may hold values from -6 to 6
- coords: bfloat16 [3, 524288], P(None, ('group', 'dom')), may hold values from 0 to 1
- msg_cot: bfloat16 [524288, 128], P(('group', 'dom')), may hold values from -6 to 6
- send_list: int32 [256, 4, 2], P(('group', 'dom')), may hold values from 0 to 15
- tiles: int32 [256, 96, 2], P(('group', 'dom')), may hold values from 0 to 23, as said below
- tile_count: int32 [256], P(('group', 'dom')), may hold values from 24 to 96, as said below
- wavevec: int32 [512, 3], replicated, may hold values from -4 to 4
- w_rad_a: bfloat16 [128, 128], replicated, may hold values from -0.5 to 0.5
- w_rad_b: bfloat16 [128, 128], replicated, may hold values from -0.5 to 0.5
- w_charge: bfloat16 [128, 128], replicated, may hold values from -0.5 to 0.5
- w_long: bfloat16 [128, 128], replicated, may hold values from -0.5 to 0.5
- norm_gain: float32 [128], replicated, may hold values from 0.1 to 1.9
- w_in: bfloat16 [128, 256], replicated, may hold values from -0.5 to 0.5
- w_out: bfloat16 [256, 128], replicated, may hold values from -0.375 to 0.375
Outputs:
- new_feats: bfloat16 [524288, 128], P(('group', 'dom'))
- feat_adjoint: float32 [524288, 128], P(('group', 'dom'))
The draws below stay inside these ranges and needn't reach their ends.
Inputs may be any that keep to these rules, and one draw needn't show every extreme that they name: In every domain the first 8 tiles have source blocks 16, 17, ... in order, one each; targets are below 16 and sources below 24. `tile_count`: tiles at or after a domain's count are not used; some domain has all 96 live.
All inputs are finite; a program needn't handle non-finite values.
Results may differ from the reference program's by a relative error of at most 0.0067.
Values may be sent and summed in bfloat16 or wider, within the bound.
A program may use at most 64 MiB of HBM per device.

```python
import jax
import jax.numpy as jnp
from jax import lax

F = 128
QC = 128
HID = 256
K = 512
BLK = 128
HB = 2
ATOMS_DEV = 2048
NBLK = 16
MAXT = 96
ATOMS = 524288
N_GROUP = 8
N_DOM = 32
DEVICES = 256


def draw_tiles(key, part):
    target = jax.random.randint(jax.random.fold_in(key, 11), (DEVICES, MAXT), 0, NBLK)
    source = jax.random.randint(jax.random.fold_in(key, 12), (DEVICES, MAXT), 0, NBLK + 4 * HB)
    ordinal = jnp.arange(MAXT, dtype=jnp.int32)
    source = jnp.where(ordinal[None, :] < 4 * HB, NBLK + ordinal[None, :], source)
    return jnp.stack([target, source], axis=-1).astype(jnp.int32)


def draw_tile_count(key, part):
    lowest = MAXT // 4
    span = MAXT - lowest + 1
    rolled = jax.random.randint(jax.random.fold_in(key, 21), (DEVICES,), 0, span)
    count = lowest + rolled * rolled * rolled // (span * span)
    busiest = jax.random.randint(jax.random.fold_in(key, 22), (), 0, DEVICES)
    count = jnp.where(jnp.arange(DEVICES) == busiest, MAXT, count)
    return count.astype(jnp.int32)


def plant(drawn, key, least, high):
    shape = drawn.shape
    spot = [jax.random.randint(jax.random.fold_in(key, axis), (), 0, shape[axis]) for axis in range(len(shape))]
    drawn = drawn.at[tuple(spot)].set(least)
    longest = shape.index(max(shape))
    spot[longest] = (spot[longest] + 1) % shape[longest]
    return drawn.at[tuple(spot)].set(high)


def shard_levels(own_key, dims, split, least, largest):
    loudness = 1.0
    for position, shards_of in split:
        steps = jax.random.uniform(jax.random.fold_in(jax.random.fold_in(own_key, 6), position), (shards_of,), jnp.float32, least / len(split), largest / len(split))
        loudness = loudness * jnp.repeat(jnp.exp(steps), dims[position] // shards_of).reshape((-1,) + (1,) * (len(dims) - 1 - position))
    return loudness


def bell_draw(stream_key, shape, deviation, bound, pieces=(), kind=jnp.bfloat16):
    array = deviation * jax.random.normal(stream_key, shape, jnp.float32)
    if pieces:
        array = array * shard_levels(stream_key, shape, pieces, -0.22, 0.18)
    return jnp.clip(array, -bound, bound).astype(kind)


def setup_inputs(seed: int = 0) -> dict:
    seeds = jax.random.split(jax.random.key(seed), 15)
    feats = bell_draw(seeds[0], (ATOMS, F), 1.0, 6.0, ((0, 256),))
    coords = jnp.clip(1.0 * jax.random.uniform(seeds[1], (3, ATOMS), jnp.float32) ** shard_levels(seeds[1], (3, ATOMS), ((1, 256),), -0.2, 0.2), 0.0, 1.0).astype(jnp.bfloat16)
    msg_cot = bell_draw(seeds[2], (ATOMS, F), 1.0, 6.0, ((0, 256),))
    send_list = plant(jax.random.randint(seeds[3], (DEVICES, 4, HB), 0, NBLK), jax.random.fold_in(seeds[3], 1), 0, NBLK - 1).astype(jnp.int32)
    tiles = draw_tiles(jax.random.fold_in(seeds[14], 71), 0)
    tile_count = draw_tile_count(jax.random.fold_in(seeds[14], 71), 0)
    wavevec = plant(jax.random.randint(seeds[6], (K, 3), -4, 5), jax.random.fold_in(seeds[6], 1), -4, 4).astype(jnp.int32)
    w_rad_a = bell_draw(seeds[7], (F, F), F ** -0.5, 0.5)
    w_rad_b = bell_draw(seeds[8], (F, F), F ** -0.5, 0.5)
    w_charge = bell_draw(seeds[9], (F, QC), F ** -0.5, 0.5)
    w_long = bell_draw(seeds[10], (QC, F), QC ** -0.5, 0.5)
    norm_gain = jnp.clip(1.0 + 0.18 * jax.random.normal(seeds[11], (F,), jnp.float32), 0.1, 1.9)
    w_in = bell_draw(seeds[12], (F, HID), F ** -0.5, 0.5)
    w_out = bell_draw(seeds[13], (HID, F), HID ** -0.5, 0.375)
    return {"feats": feats, "coords": coords, "msg_cot": msg_cot, "send_list": send_list, "tiles": tiles, "tile_count": tile_count, "wavevec": wavevec, "w_rad_a": w_rad_a, "w_rad_b": w_rad_b, "w_charge": w_charge, "w_long": w_long, "norm_gain": norm_gain, "w_in": w_in, "w_out": w_out}


RADIAL_A = 6.0
RADIAL_B = 30.0
MSG_SCALE = 1.0 / 32.0

def tile_pass(ext_feats, ext_xyz, cot_blocks, tiles_dev, count, w_rad_a, w_rad_b):
    extent = ext_feats.shape[0]
    flat = ext_feats.reshape(extent * BLK, F)
    proj_a = jnp.dot(flat, w_rad_a, preferred_element_type=jnp.float32).astype(jnp.bfloat16).reshape(extent, BLK, F)
    proj_b = jnp.dot(flat, w_rad_b, preferred_element_type=jnp.float32).astype(jnp.bfloat16).reshape(extent, BLK, F)

    def one_tile(step, carry):
        msg, grad_a, grad_b = carry
        target = tiles_dev[step, 0]
        source = tiles_dev[step, 1]
        live = jnp.where(step < count, jnp.float32(1.0), jnp.float32(0.0))
        diff = ext_xyz[:, target][:, :, None] - ext_xyz[:, source][:, None, :]
        dist2 = lax.optimization_barrier(jnp.sum(diff * diff, axis=0))
        ker_a = jnp.exp(-RADIAL_A * dist2).astype(jnp.bfloat16)
        ker_b = jnp.exp(-RADIAL_B * dist2).astype(jnp.bfloat16)
        term = jnp.dot(ker_a, proj_a[source], preferred_element_type=jnp.float32)
        term = term + jnp.dot(ker_b, proj_b[source], preferred_element_type=jnp.float32)
        msg = msg.at[target].add(live * term)
        back_a = jnp.dot(ker_a.T, cot_blocks[target], preferred_element_type=jnp.float32)
        back_b = jnp.dot(ker_b.T, cot_blocks[target], preferred_element_type=jnp.float32)
        grad_a = grad_a.at[source].add(live * back_a)
        grad_b = grad_b.at[source].add(live * back_b)
        return (msg, grad_a, grad_b)
    start = (jnp.zeros((NBLK, BLK, F), jnp.float32), jnp.zeros((extent, BLK, F), jnp.float32), jnp.zeros((extent, BLK, F), jnp.float32))
    msg, grad_a, grad_b = lax.fori_loop(0, MAXT, one_tile, start)
    msg = MSG_SCALE * msg
    grad_a = (MSG_SCALE * grad_a).astype(jnp.bfloat16).reshape(extent * BLK, F)
    grad_b = (MSG_SCALE * grad_b).astype(jnp.bfloat16).reshape(extent * BLK, F)
    grad_ext = jnp.dot(grad_a, w_rad_a.T, preferred_element_type=jnp.float32) + jnp.dot(grad_b, w_rad_b.T, preferred_element_type=jnp.float32)
    return (msg, grad_ext.reshape(extent, BLK, F))

def arrive(sent):
    return jnp.stack([jnp.roll(sent[:, :, 0], 1, axis=1), jnp.roll(sent[:, :, 1], -1, axis=1), jnp.roll(sent[:, :, 2], 1, axis=0), jnp.roll(sent[:, :, 3], -1, axis=0)], axis=2)

def depart(held):
    return jnp.stack([jnp.roll(held[:, :, 0], -1, axis=1), jnp.roll(held[:, :, 1], 1, axis=1), jnp.roll(held[:, :, 2], -1, axis=0), jnp.roll(held[:, :, 3], 1, axis=0)], axis=2)

def reference(feats, coords, msg_cot, send_list, tiles, tile_count, wavevec, w_rad_a, w_rad_b, w_charge, w_long, norm_gain, w_in, w_out):
    blocks = feats.reshape(N_GROUP, N_DOM, NBLK, BLK, F)
    xyz = jnp.moveaxis(coords.reshape(3, N_GROUP, N_DOM, NBLK, BLK), 0, 3)
    lists = send_list.reshape(N_GROUP, N_DOM, 4, HB)
    picked = jax.vmap(jax.vmap(lambda b, l: b[l]))(blocks, lists)
    picked_xyz = jax.vmap(jax.vmap(lambda b, l: b[l]))(xyz, lists)
    ext_feats = jnp.concatenate([blocks, arrive(picked).reshape(N_GROUP, N_DOM, 4 * HB, BLK, F)], axis=2)
    ext_xyz = jnp.concatenate([xyz, arrive(picked_xyz).reshape(N_GROUP, N_DOM, 4 * HB, 3, BLK)], axis=2)
    extent = NBLK + 4 * HB
    ext_feats = ext_feats.reshape(DEVICES, extent, BLK, F)
    ext_xyz = jnp.moveaxis(ext_xyz.reshape(DEVICES, extent, 3, BLK), 2, 1).astype(jnp.float32)
    cot_blocks = msg_cot.reshape(DEVICES, NBLK, BLK, F)

    def per_domain(items):
        return tile_pass(items[0], items[1], items[2], items[3], items[4], w_rad_a, w_rad_b)
    msg, grad_ext = lax.map(per_domain, (ext_feats, ext_xyz, cot_blocks, tiles, tile_count))
    grad_ext = grad_ext.reshape(N_GROUP, N_DOM, extent, BLK, F)
    held = grad_ext[:, :, NBLK:].reshape(N_GROUP, N_DOM, 4, HB, BLK, F)
    returned = depart(held).reshape(N_GROUP, N_DOM, 4 * HB, BLK, F)
    place = jax.nn.one_hot(lists.reshape(N_GROUP, N_DOM, 4 * HB), NBLK, dtype=jnp.float32)
    adjoint = grad_ext[:, :, :NBLK] + jnp.einsum('gdhb,gdhif->gdbif', place, returned, precision=lax.Precision.HIGHEST)
    feat_adjoint = adjoint.reshape(ATOMS, F)
    wave = wavevec.astype(jnp.float32)
    norm2 = lax.optimization_barrier(jnp.sum(wave * wave, axis=1))
    strength = jnp.exp(-norm2 / 16.0) / (1.0 + norm2) * float(ATOMS_DEV * N_DOM) ** (-0.5)
    group_atoms = N_DOM * ATOMS_DEV
    frac_groups = jnp.moveaxis(coords.astype(jnp.float32).reshape(3, N_GROUP, group_atoms), 1, 0)
    feat_groups = feats.reshape(N_GROUP, group_atoms, F)

    def per_group(items):
        frac, gfeats = items
        phase = 2.0 * jnp.pi * (frac[0][:, None] * wave[:, 0][None, :] + frac[1][:, None] * wave[:, 1][None, :] + frac[2][:, None] * wave[:, 2][None, :])
        cos_t = jnp.cos(phase).astype(jnp.bfloat16)
        sin_t = jnp.sin(phase).astype(jnp.bfloat16)
        charges = jnp.dot(gfeats, w_charge, preferred_element_type=jnp.float32).astype(jnp.bfloat16)
        struct_cos = jnp.dot(cos_t.T, charges, preferred_element_type=jnp.float32)
        struct_sin = jnp.dot(sin_t.T, charges, preferred_element_type=jnp.float32)
        weight_cos = (strength[:, None] * struct_cos).astype(jnp.bfloat16)
        weight_sin = (strength[:, None] * struct_sin).astype(jnp.bfloat16)
        potential = jnp.dot(cos_t, weight_cos, preferred_element_type=jnp.float32) + jnp.dot(sin_t, weight_sin, preferred_element_type=jnp.float32)
        return jnp.dot(potential.astype(jnp.bfloat16), w_long, preferred_element_type=jnp.float32)
    long_msg = lax.map(per_group, (frac_groups, feat_groups)).reshape(ATOMS, F)
    mixed = feats.astype(jnp.float32) + msg.reshape(ATOMS, F) + long_msg
    scale = lax.rsqrt(lax.optimization_barrier(jnp.mean(mixed * mixed, axis=1, keepdims=True)) + 1e-06)
    normed = (mixed * scale * norm_gain[None, :]).astype(jnp.bfloat16)
    hidden = jax.nn.silu(jnp.dot(normed, w_in, preferred_element_type=jnp.float32)).astype(jnp.bfloat16)
    new_feats = (mixed + jnp.dot(hidden, w_out, preferred_element_type=jnp.float32)).astype(jnp.bfloat16)
    return (new_feats, feat_adjoint)
```

```python
import functools

import jax
import jax.numpy as jnp
from jax import lax
from jax.experimental import pallas as pl
from jax.experimental.pallas import tpu as pltpu
from jax.sharding import PartitionSpec as P

BLK = 128
F = 128
HB = 2
MESH = pl.DeviceIdType.MESH
F32 = jnp.float32
BF16 = jnp.bfloat16
SCALE = 1.0 / 32.0
LOG2E = 1.4426950408889634
SIN_C = (4.44288292, -7.30824569, 3.60635422, -0.84611165, 0.10982452)
COS_C = (1.4142135, -6.97885095, 5.73946038, -1.88355791, 0.31068803)
MAGIC = 12582912.0
TILE_UNROLL = 4


def nn(a, b):
    return lax.dot_general(a, b, (((1,), (0,)), ((), ())), preferred_element_type=F32)


def nt(a, b):
    return lax.dot_general(a, b, (((1,), (1,)), ((), ())), preferred_element_type=F32)


def horner(coefs, u):
    acc = coefs[-1] * u + coefs[-2]
    for c in coefs[-3::-1]:
        acc = acc * u + c
    return acc


def cos_sin_turns(t):
    r = t - ((t + MAGIC) - MAGIC)
    u = r * r
    s = horner(SIN_C, u) * r
    c = horner(COS_C, u)
    return 1.0 - s * s, s * c


def kernel(
    n_dom,
    n_group,
    slots,
    send_s,
    tiles_s,
    count_s,
    tiles_v,
    coords,
    wave,
    feats,
    cot,
    w_rad_a,
    w_rad_b,
    w_charge,
    w_long,
    norm_gain,
    w_in,
    w_out,
    out_feats,
    out_adj,
    coef,
    ya,
    xa,
    wab,
    wave16,
    sbuf,
    halo,
    rbuf,
    rrecv,
    ct,
    cst,
    sacc,
    sbf,
    srecv,
    wg,
    pj,
    kt,
    tacc,
    gacc,
    adj,
    idx_v,
    idx_s,
    idx_sem,
    halo_send,
    halo_recv,
    back_send,
    back_recv,
    rs_send,
    rs_recv,
    ag_send,
    ag_recv,
):
    me = lax.axis_index("dom")
    grp = lax.axis_index("group")
    nblk = feats.shape[0]
    extent = nblk + 4 * HB
    others = n_dom - 1
    dom_next, dom_prev = lax.rem(me + 1, n_dom), lax.rem(me + n_dom - 1, n_dom)
    grp_next, grp_prev = lax.rem(grp + 1, n_group), lax.rem(grp + n_group - 1, n_group)
    forward = ((dom_next, "dom"), (dom_prev, "dom"), (grp_next, "group"), (grp_prev, "group"))
    backward = (forward[1], forward[0], forward[3], forward[2])

    barrier = pltpu.get_barrier_semaphore()

    def greet(o, carry):
        pl.semaphore_signal(
            barrier, inc=1, device_id={"dom": lax.rem(me + o, n_dom)}, device_id_type=MESH
        )
        return carry

    lax.fori_loop(1, n_dom, greet, 0)
    for peer in (grp_next, grp_prev):
        pl.semaphore_signal(barrier, inc=1, device_id={"group": peer}, device_id_type=MESH)

    eye = (
        lax.broadcasted_iota(jnp.int32, (BLK, BLK), 0)
        == lax.broadcasted_iota(jnp.int32, (BLK, BLK), 1)
    ).astype(BF16)

    x = coords[...].astype(F32)
    x2 = x[0:1] * x[0:1] + x[1:2] * x[1:2] + x[2:3] * x[2:3]
    hi = x2.astype(BF16).astype(F32)
    mid = (x2 - hi).astype(BF16).astype(F32)
    lo = x2 - hi - mid
    atoms = nblk * BLK
    coef[0, :, :] = jnp.zeros((16, atoms), F32)
    coef[1, :, :] = jnp.zeros((16, atoms), F32)
    ones = jnp.ones((3, atoms), F32)
    coef[0, 0:3, :] = x
    coef[1, 0:3, :] = -2.0 * x
    for part, value in enumerate((hi, mid, lo)):
        coef[0, 3 + part : 4 + part, :] = value
        coef[1, 6 + part : 7 + part, :] = value
    coef[0, 6:9, :] = ones
    coef[1, 3:6, :] = ones
    for b in range(nblk):
        cols = slice(b * BLK, (b + 1) * BLK)
        ya[b, :, :] = coef[1, :, cols].astype(BF16)
        xa[b, :, :] = nt(eye, coef[0, :, cols].astype(BF16)).astype(BF16)

    for d in range(4):
        for h in range(HB):
            pick = send_s[h, d]
            sbuf[d, h, 0:BLK, :] = feats[pick]
            sbuf[d, h, BLK : BLK + 16, :] = ya[pick]

    sub = lax.broadcasted_iota(jnp.int32, (BLK, BLK), 0)
    lane = lax.broadcasted_iota(jnp.int32, (BLK, BLK), 1)
    lane_row = lax.broadcasted_iota(jnp.int32, (1, BLK), 1)

    def chains(row, live_rows):
        row = jnp.broadcast_to(row, (BLK, BLK))
        col = row.T
        before = (col == row) & (sub < lane)
        prev = jnp.max(jnp.where(before, sub + 1, 0), axis=0, keepdims=True)
        alive = (col == lane) & (sub < live_rows)
        last = jnp.max(jnp.where(alive, sub + 1, 0), axis=0, keepdims=True)
        return prev, last

    idx_v[...] = jnp.full((8, BLK), -1, jnp.int32)
    idx_v[0:2, 0:slots] = tiles_v[...]
    count = count_s[0]
    prev_t, last_t = chains(idx_v[0:1, :], count)
    prev_s, last_s = chains(idx_v[1:2, :], count)
    list_row = jnp.full((1, BLK), -1, jnp.int32)
    for d in range(4):
        for h in range(HB):
            list_row = jnp.where(lane_row == d * HB + h, send_s[h, d], list_row)
    prev_l, last_l = chains(list_row, 4 * HB)
    prev_l = jnp.where(prev_l > 0, prev_l + (nblk - 1), list_row)
    last_l = jnp.where(last_l > 0, last_l + (nblk - 1), lane_row)
    for r, row in enumerate((prev_t, prev_s, last_t, last_s, prev_l, last_l)):
        idx_v[r : r + 1, :] = row
    index_copy = pltpu.make_async_copy(idx_v, idx_s, idx_sem)
    index_copy.start()

    wct = nt(eye, w_charge[...]).astype(BF16)
    wab[:, 0:F] = w_rad_a[...]
    wab[:, F : 2 * F] = w_rad_b[...]
    waves = wave[...].astype(F32)
    n_k = waves.shape[1]
    half = n_k // 2
    wave16[...] = jnp.zeros((16, n_k), F32)
    wave16[0:3, :] = waves

    def local_block(b, carry):
        block = feats[b]
        ct[b] = nt(wct, block).astype(BF16)
        both = nn(block, wab[...]).astype(BF16)
        pj[b, 0:BLK, :] = both[:, 0:F]
        pj[b, BLK : 2 * BLK, :] = both[:, F : 2 * F]
        kt[b] = nt(eye, cot[b]).astype(BF16)
        return carry

    lax.fori_loop(0, nblk, local_block, 0)

    sacc[...] = jnp.zeros_like(sacc)

    def structure(b, carry):
        rows = pl.ds(pl.multiple_of(b * BLK, BLK), BLK)
        left = xa[b]
        for q in range(n_k // BLK):
            turns = nn(left, wave16[:, q * BLK : (q + 1) * BLK].astype(BF16))
            c, s = cos_sin_turns(turns)
            k0 = q * BLK
            base = (k0 // half) * 2 * half + k0 % half
            cst[rows, base : base + BLK] = c.astype(BF16)
            cst[rows, base + half : base + half + BLK] = s.astype(BF16)
        sacc[...] += nn(ct[b], cst[rows, :])
        return carry

    lax.fori_loop(0, nblk // 2, structure, 0)
    pl.semaphore_wait(barrier, others + 2)

    def halo_copy(d, buf, into, ways, send, recv):
        peer, axis = ways[d]
        return pltpu.make_async_remote_copy(
            src_ref=buf.at[d],
            dst_ref=into.at[d],
            send_sem=send.at[d],
            recv_sem=recv.at[d],
            device_id={axis: peer},
            device_id_type=MESH,
        )

    for d in range(4):
        halo_copy(d, sbuf, halo, forward, halo_send, halo_recv).start()

    lax.fori_loop(nblk // 2, nblk, structure, 0)

    for cb in range(4):
        sbf[cb] = sacc[:, cb * half : (cb + 1) * half].astype(BF16)

    rows16 = (4 * F) // n_dom
    per_cb = F // rows16

    def piece(buf, p):
        return buf.at[p // per_cb, pl.ds(pl.multiple_of(lax.rem(p, per_cb) * rows16, rows16), rows16), :]

    def rs_copy(o):
        peer = lax.rem(me + o, n_dom)
        return pltpu.make_async_remote_copy(
            src_ref=piece(sbf, peer),
            dst_ref=srecv.at[o - 1],
            send_sem=rs_send.at[o - 1],
            recv_sem=rs_recv.at[o - 1],
            device_id={"dom": peer},
            device_id_type=MESH,
        )

    def ag_copy(o):
        peer = lax.rem(me + o, n_dom)
        return pltpu.make_async_remote_copy(
            src_ref=piece(wg, me),
            dst_ref=piece(wg, me),
            send_sem=ag_send.at[o - 1],
            recv_sem=ag_recv.at[o - 1],
            device_id={"dom": peer},
            device_id_type=MESH,
        )

    def for_others(do):
        def step(o, carry):
            do(o)
            return carry

        lax.fori_loop(1, n_dom, step, 0)

    for_others(lambda o: rs_copy(o).start())

    index_copy.wait()
    for d in range(4):
        halo_copy(d, sbuf, halo, forward, halo_send, halo_recv).wait()
    for d in range(4):
        for h in range(HB):
            e = nblk + d * HB + h
            ya[e] = halo[d, h, BLK : BLK + 16, :]
            both = nn(halo[d, h, 0:BLK, :], wab[...]).astype(BF16)
            pj[e, 0:BLK, :] = both[:, 0:F]
            pj[e, BLK : 2 * BLK, :] = both[:, F : 2 * F]

    tacc[0] = jnp.zeros((BLK, F), F32)
    gacc[0] = jnp.zeros((F, 2 * BLK), F32)

    def slot(r, t, most):
        return jnp.clip(idx_s[r, t], 0, most)

    def tile(t):
        i = tiles_s[0, t]
        j = tiles_s[1, t]
        dist2 = nn(xa[i], ya[j])
        ka = jnp.exp2(dist2 * (-6.0 * LOG2E))
        k2 = ka * ka
        kb = (k2 * k2) * ka
        kk = jnp.concatenate([ka.astype(BF16), kb.astype(BF16)], axis=1)
        tacc[t + 1] = tacc[slot(0, t, slots)] + nn(kk, pj[j])
        gacc[t + 1] = gacc[slot(1, t, slots)] + nn(kt[i], kk)

    def tile_step(step, carry):
        for u in range(TILE_UNROLL):
            tile(step * TILE_UNROLL + u)
        return carry

    steps = slots // TILE_UNROLL
    lax.fori_loop(0, steps // 2, tile_step, 0)

    for_others(lambda o: rs_copy(o).wait_recv())
    row_cb = me // per_cb
    row_in = pl.multiple_of(lax.rem(me, per_cb) * rows16, rows16)
    total = sbf[row_cb, pl.ds(row_in, rows16), :].astype(F32)
    total = total + jnp.sum(srecv[...].astype(F32), axis=0)
    norm2 = waves[0:1] * waves[0:1] + waves[1:2] * waves[1:2] + waves[2:3] * waves[2:3]
    strength = jnp.exp(norm2 * (-1.0 / 16.0)) / (1.0 + norm2) * float(atoms * n_dom) ** (-0.5)
    strength = jnp.where(me // (2 * per_cb) == 0, strength[:, 0:half], strength[:, half : 2 * half])
    wg[row_cb, pl.ds(row_in, rows16), :] = (total * strength).astype(BF16)
    for_others(lambda o: ag_copy(o).start())

    lax.fori_loop(steps // 2, steps, tile_step, 0)

    def grad_block(e):
        g = (gacc[slot(3, e, slots)] * SCALE).astype(BF16)
        rows = jnp.concatenate([nt(eye, g[:, 0:BLK]), nt(eye, g[:, BLK : 2 * BLK])], axis=1)
        return nt(rows.astype(BF16), wab[...])

    for d in range(4):
        for h in range(HB):
            rbuf[d, h] = grad_block(nblk + d * HB + h).astype(BF16)
    for d in range(4):
        halo_copy(d, rbuf, rrecv, backward, back_send, back_recv).start()

    def own_grad(b, carry):
        adj[b] = grad_block(b)
        return carry

    lax.fori_loop(0, nblk, own_grad, 0)

    for_others(lambda o: ag_copy(o).wait_recv())

    gain = norm_gain[...]

    def update(b, carry):
        pot = None
        for cb in range(4):
            rows = pl.ds(pl.multiple_of(b * 2 * BLK, 2 * BLK), 2 * BLK)
            term = nt(cst[rows, cb * half : (cb + 1) * half], wg[cb])
            pot = term if pot is None else pot + term
        long_msg = nn(pot.astype(BF16), w_long[...])
        msg = jnp.concatenate([tacc[slot(2, 2 * b, slots)], tacc[slot(2, 2 * b + 1, slots)]], axis=0) * SCALE
        own = jnp.concatenate([feats[2 * b], feats[2 * b + 1]], axis=0).astype(F32)
        mixed = own + msg + long_msg
        scale = lax.rsqrt(jnp.mean(mixed * mixed, axis=1, keepdims=True) + 1e-06)
        normed = (mixed * scale * gain).astype(BF16)
        pre = nn(normed, w_in[...])
        hidden = (pre * (0.5 + 0.5 * jnp.tanh(0.5 * pre))).astype(BF16)
        new = (mixed + nn(hidden, w_out[...])).astype(BF16)
        out_feats[2 * b] = new[0:BLK]
        out_feats[2 * b + 1] = new[BLK : 2 * BLK]
        return carry

    lax.fori_loop(0, nblk // 2, update, 0)

    for d in range(4):
        halo_copy(d, rbuf, rrecv, backward, back_send, back_recv).wait()
    for k in range(4 * HB):
        adj[nblk + k] = adj[slot(4, k, extent - 1)] + rrecv[k // HB, k % HB].astype(F32)

    def finish(b, carry):
        out_adj[b] = adj[slot(5, b, extent - 1)]
        return carry

    lax.fori_loop(0, nblk, finish, 0)
    for_others(lambda o: rs_copy(o).wait_send())
    for_others(lambda o: ag_copy(o).wait_send())


def solution(mesh):
    n_dom, n_group = mesh.shape["dom"], mesh.shape["group"]

    def body(
        feats,
        coords,
        msg_cot,
        send_list,
        tiles,
        tile_count,
        wavevec,
        w_rad_a,
        w_rad_b,
        w_charge,
        w_long,
        norm_gain,
        w_in,
        w_out,
    ):
        atoms = feats.shape[0]
        nblk = atoms // BLK
        extent = nblk + 4 * HB
        slots = tiles.shape[1]
        n_k = wavevec.shape[0]
        half = n_k // 2
        rows16 = (4 * F) // n_dom
        vmem = pl.BlockSpec(memory_space=pltpu.VMEM)
        smem = pl.BlockSpec(memory_space=pltpu.SMEM)
        tiles_t = tiles[0].T
        dma = pltpu.SemaphoreType.DMA
        new_feats, adjoint = pl.pallas_call(
            functools.partial(kernel, n_dom, n_group, slots),
            out_shape=(
                jax.ShapeDtypeStruct((nblk, BLK, F), BF16),
                jax.ShapeDtypeStruct((nblk, BLK, F), F32),
            ),
            in_specs=[smem, smem, smem] + [vmem] * 12,
            out_specs=(vmem, vmem),
            scratch_shapes=[
                pltpu.VMEM((2, 16, atoms), F32),
                pltpu.VMEM((extent, 16, BLK), BF16),
                pltpu.VMEM((nblk, BLK, 16), BF16),
                pltpu.VMEM((F, 2 * F), BF16),
                pltpu.VMEM((16, n_k), F32),
                pltpu.VMEM((4, HB, BLK + 16, F), BF16),
                pltpu.VMEM((4, HB, BLK + 16, F), BF16),
                pltpu.VMEM((4, HB, BLK, F), BF16),
                pltpu.VMEM((4, HB, BLK, F), BF16),
                pltpu.VMEM((nblk, F, BLK), BF16),
                pltpu.VMEM((atoms, 2 * n_k), BF16),
                pltpu.VMEM((F, 2 * n_k), F32),
                pltpu.VMEM((4, F, half), BF16),
                pltpu.VMEM((n_dom - 1, rows16, half), BF16),
                pltpu.VMEM((4, F, half), BF16),
                pltpu.VMEM((extent, 2 * BLK, F), BF16),
                pltpu.VMEM((nblk, F, BLK), BF16),
                pltpu.VMEM((slots + 1, BLK, F), F32),
                pltpu.VMEM((slots + 1, F, 2 * BLK), F32),
                pltpu.VMEM((extent, BLK, F), F32),
                pltpu.VMEM((8, BLK), jnp.int32),
                pltpu.SMEM((8, BLK), jnp.int32),
                dma,
                dma((4,)),
                dma((4,)),
                dma((4,)),
                dma((4,)),
                dma((n_dom - 1,)),
                dma((n_dom - 1,)),
                dma((n_dom - 1,)),
                dma((n_dom - 1,)),
            ],
            compiler_params=pltpu.CompilerParams(
                collective_id=0, has_side_effects=True, vmem_limit_bytes=58 << 20
            ),
        )(
            send_list[0].T,
            tiles_t,
            tile_count,
            tiles_t,
            coords,
            wavevec.T,
            feats.reshape(nblk, BLK, F),
            msg_cot.reshape(nblk, BLK, F),
            w_rad_a,
            w_rad_b,
            w_charge,
            w_long,
            norm_gain.reshape(1, F),
            w_in,
            w_out,
        )
        return new_feats.reshape(atoms, F), adjoint.reshape(atoms, F)

    return jax.shard_map(
        body,
        mesh=mesh,
        in_specs=(
            P(("group", "dom"), None),
            P(None, ("group", "dom")),
            P(("group", "dom"), None),
            P(("group", "dom"), None, None),
            P(("group", "dom"), None, None),
            P(("group", "dom")),
            P(),
            P(),
            P(),
            P(),
            P(),
            P(),
            P(),
            P(),
        ),
        out_specs=(P(("group", "dom"), None), P(("group", "dom"), None)),
        check_vma=False,
    )
```

```python
import functools

import jax
import jax.numpy as jnp
from jax import lax
from jax.experimental import pallas as pl
from jax.experimental.pallas import tpu as pltpu
from jax.sharding import PartitionSpec as P

BLK = 128
F = 128
HB = 2
MESH = pl.DeviceIdType.MESH
F32 = jnp.float32
BF16 = jnp.bfloat16
SCALE = 1.0 / 32.0
LOG2E = 1.4426950408889634
SIN_C = (4.44288292, -7.30824569, 3.60635422, -0.84611165, 0.10982452)
COS_C = (1.4142135, -6.97885095, 5.73946038, -1.88355791, 0.31068803)
MAGIC = 12582912.0
GROUP = 4
CHUNK = 4


def nn(a, b):
    return lax.dot_general(a, b, (((1,), (0,)), ((), ())), preferred_element_type=F32)


def nt(a, b):
    return lax.dot_general(a, b, (((1,), (1,)), ((), ())), preferred_element_type=F32)


def horner(coefs, u):
    acc = coefs[-1] * u + coefs[-2]
    for c in coefs[-3::-1]:
        acc = acc * u + c
    return acc


def cos_sin_turns(t):
    r = t - ((t + MAGIC) - MAGIC)
    u = r * r
    s = horner(SIN_C, u) * r
    c = horner(COS_C, u)
    return 1.0 - s * s, s * c


def kernel(
    n_dom,
    n_group,
    slots,
    send_s,
    tiles_s,
    count_s,
    tiles_v,
    coords,
    wave,
    feats,
    cot,
    w_rad_a,
    w_rad_b,
    w_charge,
    w_long,
    norm_gain,
    w_in,
    w_out,
    out_feats,
    out_adj,
    coef,
    ya,
    xa,
    wab,
    wave16,
    sbuf,
    halo,
    rbuf,
    rrecv,
    cst,
    sacc,
    sbf,
    srecv,
    wg,
    pj,
    kt,
    tacc,
    gacc,
    adj,
    keven,
    kodd,
    wgt,
    idx_v,
    idx_s,
    idx_sem,
    halo_send,
    halo_recv,
    back_send,
    back_recv,
    rs_send,
    rs_recv,
    ag_send,
    ag_recv,
):
    me = lax.axis_index("dom")
    grp = lax.axis_index("group")
    nblk = feats.shape[0]
    extent = nblk + 4 * HB
    others = n_dom - 1
    dom_next, dom_prev = lax.rem(me + 1, n_dom), lax.rem(me + n_dom - 1, n_dom)
    grp_next, grp_prev = lax.rem(grp + 1, n_group), lax.rem(grp + n_group - 1, n_group)
    forward = ((dom_next, "dom"), (dom_prev, "dom"), (grp_next, "group"), (grp_prev, "group"))
    backward = (forward[1], forward[0], forward[3], forward[2])

    barrier = pltpu.get_barrier_semaphore()

    def greet(o, carry):
        pl.semaphore_signal(
            barrier, inc=1, device_id={"dom": lax.rem(me + o, n_dom)}, device_id_type=MESH
        )
        return carry

    lax.fori_loop(1, n_dom, greet, 0)
    for peer in (grp_next, grp_prev):
        pl.semaphore_signal(barrier, inc=1, device_id={"group": peer}, device_id_type=MESH)

    eye = (
        lax.broadcasted_iota(jnp.int32, (BLK, BLK), 0)
        == lax.broadcasted_iota(jnp.int32, (BLK, BLK), 1)
    ).astype(BF16)

    x = coords[...].astype(F32)
    x2 = x[0:1] * x[0:1] + x[1:2] * x[1:2] + x[2:3] * x[2:3]
    hi = x2.astype(BF16).astype(F32)
    mid = (x2 - hi).astype(BF16).astype(F32)
    lo = x2 - hi - mid
    atoms = nblk * BLK
    coef[0, :, :] = jnp.zeros((16, atoms), F32)
    coef[1, :, :] = jnp.zeros((16, atoms), F32)
    ones = jnp.ones((3, atoms), F32)
    coef[0, 0:3, :] = x
    coef[1, 0:3, :] = -2.0 * x
    for part, value in enumerate((hi, mid, lo)):
        coef[0, 3 + part : 4 + part, :] = value
        coef[1, 6 + part : 7 + part, :] = value
    coef[0, 6:9, :] = ones
    coef[1, 3:6, :] = ones
    for b in range(nblk):
        cols = slice(b * BLK, (b + 1) * BLK)
        ya[b, :, :] = coef[1, :, cols].astype(BF16)
        aug = coef[0, :, cols].astype(BF16)
        pad = jnp.zeros((16, BLK), BF16)
        turned = nt(eye, jnp.concatenate([aug, pad, pad, aug], axis=0)).astype(BF16)
        xa[0, b, :, :] = turned[:, 0:32]
        xa[1, b, :, :] = turned[:, 32:64]

    for d in range(4):
        for h in range(HB):
            pick = send_s[h, d]
            sbuf[d, h, 0:BLK, :] = feats[pick]
            sbuf[d, h, BLK : BLK + 16, :] = ya[pick]

    sub = lax.broadcasted_iota(jnp.int32, (BLK, BLK), 0)
    lane = lax.broadcasted_iota(jnp.int32, (BLK, BLK), 1)
    lane_row = lax.broadcasted_iota(jnp.int32, (1, BLK), 1)

    def chains(row, live_rows):
        row = jnp.broadcast_to(row, (BLK, BLK))
        col = row.T
        before = (col == row) & (sub < lane)
        prev = jnp.max(jnp.where(before, sub + 1, 0), axis=0, keepdims=True)
        alive = (col == lane) & (sub < live_rows)
        last = jnp.max(jnp.where(alive, sub + 1, 0), axis=0, keepdims=True)
        return prev, last

    idx_v[...] = jnp.full((8, BLK), -1, jnp.int32)
    idx_v[0:2, 0:slots] = tiles_v[...]
    count = count_s[0]
    prev_t, last_t = chains(idx_v[0:1, :], count)
    prev_s, last_s = chains(idx_v[1:2, :], count)
    list_row = jnp.full((1, BLK), -1, jnp.int32)
    for d in range(4):
        for h in range(HB):
            list_row = jnp.where(lane_row == d * HB + h, send_s[h, d], list_row)
    prev_l, last_l = chains(list_row, 4 * HB)
    prev_l = jnp.where(prev_l > 0, prev_l + (nblk - 1), list_row)
    last_l = jnp.where(last_l > 0, last_l + (nblk - 1), lane_row)
    for r, row in enumerate((prev_t, prev_s, last_t, last_s, prev_l, last_l)):
        idx_v[r : r + 1, :] = row
    index_copy = pltpu.make_async_copy(idx_v, idx_s, idx_sem)
    index_copy.start()

    wct = nt(eye, w_charge[...]).astype(BF16)
    wab[:, 0:F] = w_rad_a[...]
    wab[:, F : 2 * F] = w_rad_b[...]
    waves = wave[...].astype(F32)
    n_k = waves.shape[1]
    half = n_k // 2
    wave16[...] = jnp.zeros((32, n_k), F32)
    wave16[0:3, :] = waves

    sacc[...] = jnp.zeros_like(sacc)

    def structure(step, carry):
        first = step * 2
        pair = feats[pl.ds(first, 2)].reshape(2 * BLK, F)
        both = nn(pair, wab[...]).astype(BF16)
        for sub_b in range(2):
            here = slice(sub_b * BLK, (sub_b + 1) * BLK)
            pj[first + sub_b, 0:BLK, :] = both[here, 0:F]
            pj[first + sub_b, BLK : 2 * BLK, :] = both[here, F : 2 * F]
            kt[first + sub_b] = nt(eye, cot[first + sub_b]).astype(BF16)
        charges = nt(wct, pair).astype(BF16)
        for sub_b in range(2):
            left = xa[0, first + sub_b]
            rows = pl.ds(pl.multiple_of((first + sub_b) * BLK, BLK), BLK)
            for q in range(n_k // BLK):
                turns = nn(left, wave16[:, q * BLK : (q + 1) * BLK].astype(BF16))
                c, s = cos_sin_turns(turns)
                k0 = q * BLK
                base = (k0 // half) * 2 * half + k0 % half
                cst[rows, base : base + BLK] = c.astype(BF16)
                cst[rows, base + half : base + half + BLK] = s.astype(BF16)
        two_rows = pl.ds(pl.multiple_of(first * BLK, 2 * BLK), 2 * BLK)
        sacc[...] += nn(charges, cst[two_rows, :])
        return carry

    lax.fori_loop(0, nblk // 4, structure, 0)
    pl.semaphore_wait(barrier, others + 2)

    def halo_copy(d, buf, into, ways, send, recv):
        peer, axis = ways[d]
        return pltpu.make_async_remote_copy(
            src_ref=buf.at[d],
            dst_ref=into.at[d],
            send_sem=send.at[d],
            recv_sem=recv.at[d],
            device_id={axis: peer},
            device_id_type=MESH,
        )

    for d in range(4):
        halo_copy(d, sbuf, halo, forward, halo_send, halo_recv).start()

    lax.fori_loop(nblk // 4, nblk // 2, structure, 0)

    for cb in range(4):
        sbf[cb] = sacc[:, cb * half : (cb + 1) * half].astype(BF16)

    rows16 = (4 * F) // n_dom
    per_cb = F // rows16

    def piece(buf, p):
        return buf.at[p // per_cb, pl.ds(pl.multiple_of(lax.rem(p, per_cb) * rows16, rows16), rows16), :]

    def rs_copy(o):
        peer = lax.rem(me + o, n_dom)
        return pltpu.make_async_remote_copy(
            src_ref=piece(sbf, peer),
            dst_ref=srecv.at[o - 1],
            send_sem=rs_send.at[o - 1],
            recv_sem=rs_recv.at[o - 1],
            device_id={"dom": peer},
            device_id_type=MESH,
        )

    def ag_copy(o):
        peer = lax.rem(me + o, n_dom)
        return pltpu.make_async_remote_copy(
            src_ref=piece(wg, me),
            dst_ref=piece(wg, me),
            send_sem=ag_send.at[o - 1],
            recv_sem=ag_recv.at[o - 1],
            device_id={"dom": peer},
            device_id_type=MESH,
        )

    def for_others(do):
        def step(o, carry):
            do(o)
            return carry

        lax.fori_loop(1, n_dom, step, 0)

    for_others(lambda o: rs_copy(o).start())

    index_copy.wait()
    for d in range(4):
        halo_copy(d, sbuf, halo, forward, halo_send, halo_recv).wait()
    for d in range(4):
        for h in range(HB):
            e = nblk + d * HB + h
            ya[e] = halo[d, h, BLK : BLK + 16, :]
            both = nn(halo[d, h, 0:BLK, :], wab[...]).astype(BF16)
            pj[e, 0:BLK, :] = both[:, 0:F]
            pj[e, BLK : 2 * BLK, :] = both[:, F : 2 * F]

    tacc[0] = jnp.zeros((BLK, F), F32)
    gacc[0] = jnp.zeros((F, 2 * BLK), F32)

    def slot(r, t, most):
        return jnp.clip(idx_s[r, t], 0, most)

    def make_kernels(buf, group):
        group = jnp.minimum(group, groups - 1)
        zero = jnp.zeros((16, BLK), BF16)
        for u in range(0, GROUP, 2):
            t = group * GROUP + u
            left = xa[0, tiles_s[0, t]] + xa[1, tiles_s[0, t + 1]]
            top = jnp.concatenate([ya[tiles_s[1, t]], zero], axis=1)
            low = jnp.concatenate([zero, ya[tiles_s[1, t + 1]]], axis=1)
            dist2 = nn(left, jnp.concatenate([top, low], axis=0))
            ka = jnp.exp2(dist2 * (-6.0 * LOG2E))
            k2 = ka * ka
            kb = (k2 * k2) * ka
            ka = ka.astype(BF16)
            kb = kb.astype(BF16)
            for v in range(2):
                here = slice(v * BLK, (v + 1) * BLK)
                buf[u + v, :, 0:BLK] = ka[:, here]
                buf[u + v, :, BLK : 2 * BLK] = kb[:, here]

    def use_kernels(buf, group):
        for u in range(GROUP):
            t = group * GROUP + u
            kk = buf[u]
            term = nn(kk, pj[tiles_s[1, t]])
            back = nn(kt[tiles_s[0, t]], kk)
            tacc[t + 1] = tacc[slot(0, t, slots)] + term
            gacc[t + 1] = gacc[slot(1, t, slots)] + back

    def tile_step(step, carry):
        make_kernels(kodd, 2 * step + 1)
        use_kernels(keven, 2 * step)
        make_kernels(keven, 2 * step + 2)
        use_kernels(kodd, 2 * step + 1)
        return carry

    groups = slots // GROUP
    steps = groups // 2
    make_kernels(keven, 0)
    lax.fori_loop(0, steps // 2, tile_step, 0)

    for_others(lambda o: rs_copy(o).wait_recv())
    row_cb = me // per_cb
    row_in = pl.multiple_of(lax.rem(me, per_cb) * rows16, rows16)
    total = sbf[row_cb, pl.ds(row_in, rows16), :].astype(F32)
    total = total + jnp.sum(srecv[...].astype(F32), axis=0)
    norm2 = waves[0:1] * waves[0:1] + waves[1:2] * waves[1:2] + waves[2:3] * waves[2:3]
    strength = jnp.exp(norm2 * (-1.0 / 16.0)) / (1.0 + norm2) * float(atoms * n_dom) ** (-0.5)
    strength = jnp.where(me // (2 * per_cb) == 0, strength[:, 0:half], strength[:, half : 2 * half])
    wg[row_cb, pl.ds(row_in, rows16), :] = (total * strength).astype(BF16)
    for_others(lambda o: ag_copy(o).start())

    lax.fori_loop(steps // 2, steps, tile_step, 0)

    def grad_block(e):
        g = (gacc[slot(3, e, slots)] * SCALE).astype(BF16)
        return nn(wab[...], jnp.concatenate([g[:, 0:BLK], g[:, BLK : 2 * BLK]], axis=0))

    for d in range(4):
        for h in range(HB):
            rbuf[d, h] = grad_block(nblk + d * HB + h).astype(BF16)
    for d in range(4):
        halo_copy(d, rbuf, rrecv, backward, back_send, back_recv).start()

    def own_grad(b, carry):
        adj[b] = grad_block(b)
        return carry

    lax.fori_loop(0, nblk, own_grad, 0)

    for_others(lambda o: ag_copy(o).wait_recv())

    gain = norm_gain[...]

    wide_eye = (
        lax.broadcasted_iota(jnp.int32, (half, half), 0)
        == lax.broadcasted_iota(jnp.int32, (half, half), 1)
    ).astype(BF16)
    for cb in range(4):
        wgt[cb] = nt(wide_eye, wg[cb]).astype(BF16)

    def update(step, carry):
        rows = pl.ds(pl.multiple_of(step * CHUNK * BLK, CHUNK * BLK), CHUNK * BLK)
        pot = None
        for cb in range(4):
            term = nn(cst[rows, cb * half : (cb + 1) * half], wgt[cb])
            pot = term if pot is None else pot + term
        long_msg = nn(pot.astype(BF16), w_long[...])
        first = step * CHUNK
        msg = jnp.concatenate(
            [tacc[slot(2, first + v, slots)] for v in range(CHUNK)], axis=0
        )
        own = feats[pl.ds(first, CHUNK)].reshape(CHUNK * BLK, F).astype(F32)
        mixed = own + msg * SCALE + long_msg
        scale = lax.rsqrt(jnp.mean(mixed * mixed, axis=1, keepdims=True) + 1e-06)
        normed = (mixed * scale * gain).astype(BF16)
        pre = nn(normed, w_in[...])
        hidden = (pre * (0.5 + 0.5 * jnp.tanh(0.5 * pre))).astype(BF16)
        new = (mixed + nn(hidden, w_out[...])).astype(BF16)
        out_feats[pl.ds(first, CHUNK)] = new.reshape(CHUNK, BLK, F)
        return carry

    lax.fori_loop(0, nblk // CHUNK, update, 0)

    for d in range(4):
        halo_copy(d, rbuf, rrecv, backward, back_send, back_recv).wait()
    for k in range(4 * HB):
        adj[nblk + k] = adj[slot(4, k, extent - 1)] + rrecv[k // HB, k % HB].astype(F32)

    def finish(b, carry):
        out_adj[b] = adj[slot(5, b, extent - 1)].T
        return carry

    lax.fori_loop(0, nblk, finish, 0)
    for_others(lambda o: rs_copy(o).wait_send())
    for_others(lambda o: ag_copy(o).wait_send())


def solution(mesh):
    n_dom, n_group = mesh.shape["dom"], mesh.shape["group"]

    def body(
        feats,
        coords,
        msg_cot,
        send_list,
        tiles,
        tile_count,
        wavevec,
        w_rad_a,
        w_rad_b,
        w_charge,
        w_long,
        norm_gain,
        w_in,
        w_out,
    ):
        atoms = feats.shape[0]
        nblk = atoms // BLK
        extent = nblk + 4 * HB
        slots = tiles.shape[1]
        n_k = wavevec.shape[0]
        half = n_k // 2
        rows16 = (4 * F) // n_dom
        vmem = pl.BlockSpec(memory_space=pltpu.VMEM)
        smem = pl.BlockSpec(memory_space=pltpu.SMEM)
        tiles_t = tiles[0].T
        dma = pltpu.SemaphoreType.DMA
        new_feats, adjoint = pl.pallas_call(
            functools.partial(kernel, n_dom, n_group, slots),
            out_shape=(
                jax.ShapeDtypeStruct((nblk, BLK, F), BF16),
                jax.ShapeDtypeStruct((nblk, BLK, F), F32),
            ),
            in_specs=[smem, smem, smem] + [vmem] * 12,
            out_specs=(vmem, vmem),
            scratch_shapes=[
                pltpu.VMEM((2, 16, atoms), F32),
                pltpu.VMEM((extent, 16, BLK), BF16),
                pltpu.VMEM((2, nblk, BLK, 32), BF16),
                pltpu.VMEM((F, 2 * F), BF16),
                pltpu.VMEM((32, n_k), F32),
                pltpu.VMEM((4, HB, BLK + 16, F), BF16),
                pltpu.VMEM((4, HB, BLK + 16, F), BF16),
                pltpu.VMEM((4, HB, BLK, F), BF16),
                pltpu.VMEM((4, HB, BLK, F), BF16),
                pltpu.VMEM((atoms, 2 * n_k), BF16),
                pltpu.VMEM((F, 2 * n_k), F32),
                pltpu.VMEM((4, F, half), BF16),
                pltpu.VMEM((n_dom - 1, rows16, half), BF16),
                pltpu.VMEM((4, F, half), BF16),
                pltpu.VMEM((extent, 2 * BLK, F), BF16),
                pltpu.VMEM((nblk, F, BLK), BF16),
                pltpu.VMEM((slots + 1, BLK, F), F32),
                pltpu.VMEM((slots + 1, F, 2 * BLK), F32),
                pltpu.VMEM((extent, F, BLK), F32),
                pltpu.VMEM((GROUP, BLK, 2 * BLK), BF16),
                pltpu.VMEM((GROUP, BLK, 2 * BLK), BF16),
                pltpu.VMEM((4, half, F), BF16),
                pltpu.VMEM((8, BLK), jnp.int32),
                pltpu.SMEM((8, BLK), jnp.int32),
                dma,
                dma((4,)),
                dma((4,)),
                dma((4,)),
                dma((4,)),
                dma((n_dom - 1,)),
                dma((n_dom - 1,)),
                dma((n_dom - 1,)),
                dma((n_dom - 1,)),
            ],
            compiler_params=pltpu.CompilerParams(
                collective_id=0, has_side_effects=True, vmem_limit_bytes=58 << 20
            ),
        )(
            send_list[0].T,
            tiles_t,
            tile_count,
            tiles_t,
            coords,
            wavevec.T,
            feats.reshape(nblk, BLK, F),
            msg_cot.reshape(nblk, BLK, F),
            w_rad_a,
            w_rad_b,
            w_charge,
            w_long,
            norm_gain.reshape(1, F),
            w_in,
            w_out,
        )
        return new_feats.reshape(atoms, F), adjoint.reshape(atoms, F)

    return jax.shard_map(
        body,
        mesh=mesh,
        in_specs=(
            P(("group", "dom"), None),
            P(None, ("group", "dom")),
            P(("group", "dom"), None),
            P(("group", "dom"), None, None),
            P(("group", "dom"), None, None),
            P(("group", "dom")),
            P(),
            P(),
            P(),
            P(),
            P(),
            P(),
            P(),
            P(),
        ),
        out_specs=(P(("group", "dom"), None), P(("group", "dom"), None)),
        check_vma=False,
    )
```
